32 devices in a mesh: sec: 4 (over y, core), brick: 8 (over z, x).
Axes of the slice: x: 2, y: 2, z: 4, core: 2. Of those that a mesh axis runs over, the one named last changes fastest.
Arguments:
- tokens: bfloat16 [64, 128, 16, 384], P(('sec', 'brick')), may hold values from -6 to 6
- tissue: int32 [8, 16, 2, 512], P('sec', 'brick'), may hold values from 0 to 1, as said below
- norm1_gain: float32 [384], replicated, may hold values from 0.1 to 1.9
- qkv_weight: bfloat16 [384, 1152], replicated, may hold values from -0.3125 to 0.3125
- position_bias: bfloat16 [12, 512, 512], replicated, may hold values from -4 to 250
- out_weight: bfloat16 [384, 384], replicated, may hold values from -0.3125 to 0.3125
- norm2_gain: float32 [384], replicated, may hold values from 0.1 to 1.9
- up_weight: bfloat16 [384, 1536], replicated, may hold values from -0.3125 to 0.3125
- down_weight: bfloat16 [1536, 384], replicated, may hold values from -0.15625 to 0.15625
Outputs:
- layer_out: bfloat16 [64, 128, 16, 384], P('sec', 'brick')
The draws below stay inside these ranges and needn't reach their ends.
Inputs may be any that keep to these rules, and one draw needn't show every extreme that they name: `tissue`: window (a, b, c) lies on the device of sec index a // 2 and brick index b // 2. Of the 8 windows of one device at most 6 hold any 1, and in every draw some device has exactly 6 such windows; every other window is all 0.
All inputs are finite; a program needn't handle non-finite values.
Results may differ from the reference program's by a relative error of at most 0.003.
Values may be sent and summed in bfloat16 or wider, within the bound.
A program may use at most 128 MiB of HBM per device.

```python
import jax
import jax.numpy as jnp
from jax import lax

D = 384
HEADS = 12
MLP_UNITS = 1536
WIN = 8
SHIFT = 4
WINDOW_TOKENS = 512
BZ = 16
BY = 16
BX = 16
LIVE_MOST = 6
VOL_Z = 64
VOL_Y = 128
VOL_X = 16
N_SEC = 4
N_BRICK = 8


def draw_tissue(key, part):
    count_z = BZ // WIN
    count_y = BY // WIN
    count_x = BX // WIN
    per_device = count_z * count_y * count_x
    devices = N_SEC * N_BRICK
    count_key, busy_key, order_key, token_key, spot_key = jax.random.split(key, 5)
    counts = jax.random.randint(count_key, (devices,), 1, max(LIVE_MOST // 2, 1) + 1)
    busiest = jax.random.randint(busy_key, (), 0, devices)
    counts = jnp.where(jnp.arange(devices) == busiest, LIVE_MOST, counts)

    def shuffled(subkey):
        return jax.random.permutation(subkey, per_device)
    window_rank = jax.vmap(shuffled)(jax.random.split(order_key, devices))
    alive_mask = window_rank < counts[:, None]
    tokens_on = jax.random.randint(token_key, (devices, per_device, WINDOW_TOKENS), 0, 4) < 3
    forced_spot = jax.random.randint(spot_key, (devices, per_device, 1), 0, WINDOW_TOKENS)
    tokens_on = tokens_on | (jnp.arange(WINDOW_TOKENS)[None, None, :] == forced_spot)
    tissue_marks = (alive_mask[:, :, None] & tokens_on).astype(jnp.int32)
    tissue_marks = tissue_marks.reshape(N_SEC, N_BRICK, count_z, count_y, count_x, WINDOW_TOKENS)
    tissue_marks = tissue_marks.transpose(0, 2, 1, 3, 4, 5)
    return tissue_marks.reshape(N_SEC * count_z, N_BRICK * count_y, count_x, WINDOW_TOKENS)


def draw_position_bias(key, part):
    shape = (HEADS, WINDOW_TOKENS, WINDOW_TOKENS)
    base_key = jax.random.fold_in(key, 0)
    return jnp.clip(jax.random.normal(base_key, shape, jnp.float32), -4.0, 4.0).astype(jnp.bfloat16)


def level_of(stream_key, extent, cuts, smallest, high):
    gain = 1.0
    for dim, blocks in cuts:
        draws = jax.random.uniform(jax.random.fold_in(jax.random.fold_in(stream_key, 6), dim), (blocks,), jnp.float32, smallest / len(cuts), high / len(cuts))
        gain = gain * jnp.repeat(jnp.exp(draws), extent[dim] // blocks).reshape((-1,) + (1,) * (len(extent) - 1 - dim))
    return gain


def noise(rng, shape, scale, most, cuts=(), dtype=jnp.bfloat16):
    entries = scale * jax.random.normal(rng, shape, jnp.float32)
    if cuts:
        entries = entries * level_of(rng, shape, cuts, -0.22, 0.18)
    return jnp.clip(entries, -most, most).astype(dtype)


def setup_inputs(seed: int = 0) -> dict:
    key_list = jax.random.split(jax.random.key(seed), 10)
    return {
        "tokens": noise(key_list[0], (VOL_Z, VOL_Y, VOL_X, D), 1.0, 6.0, ((0, 32),)),
        "tissue": draw_tissue(jax.random.fold_in(key_list[9], 71), 0),
        "norm1_gain": jnp.clip(1.0 + 0.18 * jax.random.normal(key_list[2], (D,), jnp.float32), 0.1, 1.9),
        "qkv_weight": noise(key_list[3], (D, 3 * D), D ** -0.5, 0.3125),
        "position_bias": draw_position_bias(jax.random.fold_in(key_list[9], 71), 0),
        "out_weight": noise(key_list[5], (D, D), D ** -0.5, 0.3125),
        "norm2_gain": jnp.clip(1.0 + 0.18 * jax.random.normal(key_list[6], (D,), jnp.float32), 0.1, 1.9),
        "up_weight": noise(key_list[7], (D, MLP_UNITS), D ** -0.5, 0.3125),
        "down_weight": noise(key_list[8], (MLP_UNITS, D), MLP_UNITS ** -0.5, 0.15625),
    }


EPS = 1e-05

def layer_norm(values, gain_row):
    values = values.astype(jnp.float32)
    centered = values - lax.optimization_barrier(jnp.mean(values, axis=-1, keepdims=True))
    variance = lax.optimization_barrier(jnp.mean(centered * centered, axis=-1, keepdims=True))
    return centered * lax.rsqrt(variance + EPS) * gain_row

def cut_windows(volume):
    depth_cells, height, across, features = volume.shape
    count_z, count_y, count_x = (depth_cells // WIN, height // WIN, across // WIN)
    blocks = volume.reshape(count_z, WIN, count_y, WIN, count_x, WIN, features)
    return blocks.transpose(0, 2, 4, 1, 3, 5, 6).reshape(count_z * count_y * count_x, WIN ** 3, features)

def join_windows(windows, depth_cells, height, across):
    features = windows.shape[-1]
    count_z, count_y, count_x = (depth_cells // WIN, height // WIN, across // WIN)
    blocks = windows.reshape(count_z, count_y, count_x, WIN, WIN, WIN, features)
    return blocks.transpose(0, 3, 1, 4, 2, 5, 6).reshape(depth_cells, height, across, features)

def window_block(windows, tissue_rows, labels, norm1_gain, qkv_weight, position_bias, out_weight, norm2_gain, up_weight, down_weight):
    groups, length, model_width = windows.shape
    head_count = position_bias.shape[0]
    head_size = model_width // head_count
    flat_rows = windows.reshape(groups * length, model_width)
    normed = layer_norm(flat_rows, norm1_gain).astype(jnp.bfloat16)
    projected = jnp.dot(normed, qkv_weight, preferred_element_type=jnp.float32).astype(jnp.bfloat16)
    projected = projected.reshape(groups, length, 3, head_count, head_size)
    queries = projected[:, :, 0].astype(jnp.float32)
    keys_all = projected[:, :, 1].astype(jnp.float32)
    values_all = projected[:, :, 2].astype(jnp.float32)
    scores = jnp.einsum('gqhd,gkhd->ghqk', queries, keys_all) * head_size ** (-0.5)
    scores = scores + position_bias.astype(jnp.float32)[None]
    allowed = (tissue_rows[:, None, :] == 1) & (labels[:, :, None] == labels[:, None, :])
    scores = jnp.where(allowed[:, None], scores, -1e+30)
    row_top = lax.optimization_barrier(jnp.max(scores, axis=-1, keepdims=True))
    raised = jnp.exp(scores - row_top)
    attention = (raised / lax.optimization_barrier(jnp.sum(raised, axis=-1, keepdims=True))).astype(jnp.bfloat16)
    mixed = jnp.einsum('ghqk,gkhd->gqhd', attention.astype(jnp.float32), values_all).astype(jnp.bfloat16)
    mixed = mixed.reshape(groups * length, model_width)
    attended = flat_rows.astype(jnp.float32) + jnp.dot(mixed, out_weight, preferred_element_type=jnp.float32)
    normed_two = layer_norm(attended, norm2_gain).astype(jnp.bfloat16)
    feed = jax.nn.gelu(jnp.dot(normed_two, up_weight, preferred_element_type=jnp.float32), approximate=False).astype(jnp.bfloat16)
    result = attended + jnp.dot(feed, down_weight, preferred_element_type=jnp.float32)
    keep_token = tissue_rows.reshape(groups * length, 1) == 1
    result = jnp.where(keep_token, result, flat_rows.astype(jnp.float32)).astype(jnp.bfloat16)
    return result.reshape(groups, length, model_width)

def reference(tokens, tissue, norm1_gain, qkv_weight, position_bias, out_weight, norm2_gain, up_weight, down_weight):
    depth_cells, height, across, model_width = tokens.shape
    rolled = jnp.roll(tokens, (-SHIFT, -SHIFT, -SHIFT), axis=(0, 1, 2))
    windows = cut_windows(rolled)
    count = windows.shape[0]
    depth_index = lax.broadcasted_iota(jnp.int32, (depth_cells, height, across, 1), 0)
    height_index = lax.broadcasted_iota(jnp.int32, (depth_cells, height, across, 1), 1)
    across_index = lax.broadcasted_iota(jnp.int32, (depth_cells, height, across, 1), 2)
    label_grid = 4 * (depth_index >= depth_cells - SHIFT).astype(jnp.int32)
    label_grid = label_grid + 2 * (height_index >= height - SHIFT).astype(jnp.int32)
    label_grid = label_grid + (across_index >= across - SHIFT).astype(jnp.int32)
    labels = cut_windows(label_grid)[:, :, 0]
    tissue_rows = tissue.reshape(count, WIN ** 3)
    batch = 4 if count % 4 == 0 else 1

    def one_group(packed):
        group_windows, group_tissue, group_labels = packed
        return window_block(group_windows, group_tissue, group_labels, norm1_gain, qkv_weight, position_bias, out_weight, norm2_gain, up_weight, down_weight)
    blocks = lax.map(one_group, (windows.reshape(count // batch, batch, WIN ** 3, model_width), tissue_rows.reshape(count // batch, batch, WIN ** 3), labels.reshape(count // batch, batch, WIN ** 3)))
    blocks = blocks.reshape(count, WIN ** 3, model_width)
    volume = join_windows(blocks, depth_cells, height, across)
    return jnp.roll(volume, (SHIFT, SHIFT, SHIFT), axis=(0, 1, 2))
```

```python
import functools

import jax
import jax.numpy as jnp
from jax import lax
from jax.experimental import pallas as pl
from jax.experimental.pallas import tpu as pltpu
from jax.sharding import PartitionSpec as P

WIN = 8
SHIFT = 4
EPS = 1e-05
TOKENS = WIN**3
LANES = 128
MASKED = -1e30
ROWS = 256
UNITS = 512
SQUARE = WIN * WIN
WINDOWS = 8
MESH = pl.DeviceIdType.MESH


def layer_norm(values, gain_row):
    centered = values - jnp.mean(values, axis=-1, keepdims=True)
    variance = jnp.mean(centered * centered, axis=-1, keepdims=True)
    return centered * lax.rsqrt(variance + EPS) * gain_row


def gelu(v):
    return 0.5 * v * (1.0 + lax.erf(v * (0.5**0.5)))


def slot(a, b, c):
    return 4 * (1 - b) + 2 * c + 1 - a


def block_kernel(
    tokens,
    tissue_ref,
    gain1_ref,
    qkv_hbm,
    bias_hbm,
    out_w_hbm,
    gain2_ref,
    up_hbm,
    down_hbm,
    out,
    cells,
    stage,
    recv,
    done,
    qkv_ref,
    bias_ref,
    out_w_ref,
    up_ref,
    down_ref,
    qkv,
    mix,
    key_mask,
    label_hot,
    kept,
    cells_sem,
    weight_sem,
    send_sem,
    recv_sem,
    back_send,
    back_recv,
    *,
    head_size,
    n_sec,
    n_brick,
):
    sec = lax.axis_index("sec")
    me = lax.axis_index("brick")
    planes = tokens.shape[0]
    rows = tokens.shape[1]
    width = tokens.shape[-1]
    early = SHIFT // planes
    depth = planes * n_brick
    rolled = lax.rem(planes * me + depth - SHIFT, depth)
    my_a = lax.div(rolled, WIN)
    my_plane = lax.rem(rolled, WIN)
    is_early = me < early
    to_sec = lax.rem(sec + n_sec - is_early.astype(jnp.int32), n_sec)

    barrier = pltpu.get_barrier_semaphore()

    def greet(s, b):
        pl.semaphore_signal(barrier, inc=1, device_id=(s, b), device_id_type=MESH)

    above = lax.rem(sec + 1, n_sec)
    below = lax.rem(sec + n_sec - 1, n_sec)
    right = lax.rem(me + 1, n_brick)
    left = lax.rem(me + n_brick - 1, n_brick)

    cells_copy = pltpu.make_async_copy(tokens, cells, cells_sem)
    cells_copy.start()

    @pl.loop(0, early)
    def _(k):
        greet(above, k)

    @pl.loop(early, n_brick)
    def _(k):
        @pl.when(k != me)
        def _():
            greet(sec, k)

    greet(sec, left)
    greet(below, me)
    greet(below, left)

    weight_copies = [
        pltpu.make_async_copy(source, target, weight_sem.at[i])
        for i, (source, target) in enumerate(
            (
                (qkv_hbm, qkv_ref),
                (bias_hbm, bias_ref),
                (out_w_hbm, out_w_ref),
                (up_hbm, up_ref),
                (down_hbm, down_ref),
            )
        )
    ]

    cells_copy.wait()

    def store_cut(block, m, p, at, count):
        block = pltpu.roll(block.astype(jnp.float32), 2 * WIN - SHIFT, 1)
        for c in range(2):
            part = block[:, c * WIN : (c + 1) * WIN].reshape(count * WIN, width)
            stage[m, c, p, pl.ds(at, count * WIN)] = part.astype(jnp.bfloat16)

    for p in range(planes):

        @pl.loop(0, rows // WIN - 1)
        def _(m):
            store_cut(cells[p, pl.ds(m * WIN + SHIFT, WIN)], m, p, 0, WIN)

        last = rows // WIN - 1
        store_cut(cells[p, rows - SHIFT :], last, p, 0, SHIFT)
        store_cut(cells[p, :SHIFT], last, p, SHIFT * WIN, SHIFT)

    pl.semaphore_wait(
        barrier, n_brick + 2 + is_early.astype(jnp.int32)
    )

    def piece(j, b, c):
        d = lax.rem(me + j, n_brick)
        source = stage.at[2 * d + b, c]
        target = recv.at[slot(my_a, b, c), pl.ds(my_plane, planes)]
        remote = pltpu.make_async_remote_copy(
            src_ref=source,
            dst_ref=target,
            send_sem=send_sem.at[2 * b + c, j],
            recv_sem=recv_sem.at[2 * b + c, me],
            device_id=(to_sec, d),
            device_id_type=MESH,
        )
        inside = pltpu.make_async_copy(source, target, recv_sem.at[2 * b + c, me])
        return remote, inside

    for b in (1, 0):
        for c in (0, 1):

            @pl.loop(1, n_brick)
            def _(j):
                piece(j, b, c)[0].start()

            remote, inside = piece(0, b, c)

            @pl.when(is_early)
            def _():
                remote.start()

            @pl.when(jnp.logical_not(is_early))
            def _():
                inside.start()

    for copy in weight_copies:
        copy.start()
    for copy in weight_copies:
        copy.wait()

    heads_per_group = LANES // head_size
    groups = width // LANES

    def back(t, ph, rh):
        a = 1 - lax.rem(t, 2)
        c = lax.rem(lax.div(t, 2), 2)
        b = 1 - lax.div(t, 4)
        z0 = lax.rem(SHIFT + WIN * a + SHIFT * ph, 2 * WIN)
        y0 = lax.rem(SHIFT + WIN * b + SHIFT * rh, 2 * WIN)
        source = done.at[t, pl.ds(SHIFT * ph, SHIFT), pl.ds(SHIFT * WIN * rh, SHIFT * WIN)]
        target = out.at[c, pl.ds(z0, SHIFT), pl.ds(WIN * y0, SHIFT * WIN)]
        away = a * ph + b * rh > 0
        remote = pltpu.make_async_remote_copy(
            src_ref=source,
            dst_ref=target,
            send_sem=back_send.at[t, 2 * ph + rh],
            recv_sem=back_recv.at[t, 2 * ph + rh],
            device_id=(lax.rem(sec + a * ph, n_sec), lax.rem(me + b * rh, n_brick)),
            device_id_type=MESH,
        )
        inside = pltpu.make_async_copy(source, target, back_recv.at[t, 2 * ph + rh])
        return away, remote, inside

    @pl.loop(0, WINDOWS)
    def _(t):
        a = 1 - lax.rem(t, 2)
        c = lax.rem(lax.div(t, 2), 2)
        b = 1 - lax.div(t, 4)

        for i in range(WIN // planes):
            k = lax.rem(early + a * (WIN // planes) + i, n_brick)
            here = recv.at[t, pl.ds(i * planes, planes)]
            pltpu.make_async_copy(here, here, recv_sem.at[2 * b + c, k]).wait()

        z_last = (sec == n_sec - 1).astype(jnp.int32) * a
        y_last = (me == n_brick - 1).astype(jnp.int32) * b
        token = lax.broadcasted_iota(jnp.int32, (TOKENS, LANES), 0)
        lane = lax.broadcasted_iota(jnp.int32, (TOKENS, LANES), 1)
        fz = ((token // SQUARE) >= SHIFT).astype(jnp.int32) * z_last
        fy = (((token // WIN) % WIN) >= SHIFT).astype(jnp.int32) * y_last
        fx = ((token % WIN) >= SHIFT).astype(jnp.int32) * c
        label = 4 * fz + 2 * fy + fx
        here = label == lane
        marks = tissue_ref[a, b, pl.ds(c, 1), :].astype(jnp.float32)
        marks = jnp.broadcast_to(marks.reshape(1, TOKENS), (LANES, TOKENS)).T
        kept[...] = marks
        label_hot[...] = jnp.where(here, 1.0, 0.0).astype(jnp.bfloat16)
        key_mask[...] = jnp.where(here & (marks > 0.5), 0.0, MASKED).astype(jnp.bfloat16)

        x = recv[t].reshape(TOKENS, width).astype(jnp.float32)
        normed = layer_norm(x, gain1_ref[...].reshape(1, width)).astype(jnp.bfloat16)
        scale = head_size ** (-0.5)
        qkv[:, :width] = (
            jnp.dot(normed, qkv_ref[:, :width], preferred_element_type=jnp.float32) * scale
        ).astype(jnp.bfloat16)
        for part in (1, 2):
            cols = slice(part * width, (part + 1) * width)
            qkv[:, cols] = jnp.dot(
                normed, qkv_ref[:, cols], preferred_element_type=jnp.float32
            ).astype(jnp.bfloat16)

        @pl.loop(0, groups, unroll=True)
        def _(g):
            at = pl.multiple_of(g * LANES, LANES)
            keys = jnp.concatenate(
                [qkv[:, pl.ds(pl.multiple_of(width + at, LANES), LANES)], key_mask[...]],
                axis=1,
            )
            values = jnp.concatenate(
                [
                    qkv[:, pl.ds(pl.multiple_of(2 * width + at, LANES), LANES)],
                    jnp.ones((TOKENS, LANES), jnp.bfloat16),
                ],
                axis=1,
            )
            lane_head = lax.broadcasted_iota(jnp.int32, (ROWS, LANES), 1) // head_size
            for r in range(TOKENS // ROWS):
                span = slice(r * ROWS, (r + 1) * ROWS)
                queries = qkv[span, pl.ds(at, LANES)]
                hot = label_hot[span, :]
                total = None
                for h in range(heads_per_group):
                    mine = lane_head == h
                    query = jnp.where(mine, queries, jnp.zeros_like(queries))
                    scores = lax.dot_general(
                        jnp.concatenate([query, hot], axis=1),
                        keys,
                        (((1,), (1,)), ((), ())),
                        preferred_element_type=jnp.float32,
                    )
                    scores = scores + bias_ref[g * heads_per_group + h, span, :].astype(
                        jnp.float32
                    )
                    top = jnp.max(scores, axis=-1, keepdims=True)
                    raised = jnp.exp(scores - top).astype(jnp.bfloat16)
                    got = jnp.dot(raised, values, preferred_element_type=jnp.float32)
                    value, weight = got[:, :LANES], got[:, LANES:]
                    if total is None:
                        total, sums = value, weight
                    else:
                        total = jnp.where(mine, value, total)
                        sums = jnp.where(mine, weight, sums)
                mix[span, pl.ds(at, LANES)] = (total / sums).astype(jnp.bfloat16)

        x = recv[t].reshape(TOKENS, width).astype(jnp.float32)
        attended = x + jnp.dot(mix[...], out_w_ref[...], preferred_element_type=jnp.float32)
        normed2 = layer_norm(attended, gain2_ref[...].reshape(1, width)).astype(jnp.bfloat16)
        result = attended
        for j in range(up_ref.shape[1] // UNITS):
            units = slice(j * UNITS, (j + 1) * UNITS)
            feed = gelu(
                jnp.dot(normed2, up_ref[:, units], preferred_element_type=jnp.float32)
            ).astype(jnp.bfloat16)
            result = result + jnp.dot(
                feed, down_ref[units, :], preferred_element_type=jnp.float32
            )
        keep = jnp.concatenate([kept[...]] * groups, axis=1) > 0.5
        result = jnp.where(keep, result, x).astype(jnp.bfloat16)
        done[t] = result.reshape(WIN, SQUARE, width)

        for ph in range(2):
            for rh in range(2):
                away, remote, inside = back(t, ph, rh)

                @pl.when(away)
                def _():
                    remote.start()

                @pl.when(jnp.logical_not(away))
                def _():
                    inside.start()

    for b in (1, 0):
        for c in (0, 1):

            @pl.loop(1, n_brick)
            def _(j):
                piece(j, b, c)[0].wait_send()

            remote, _ = piece(0, b, c)

            @pl.when(is_early)
            def _():
                remote.wait_send()

    @pl.loop(0, WINDOWS)
    def _(t):
        for ph in range(2):
            for rh in range(2):
                away, remote, inside = back(t, ph, rh)

                @pl.when(away)
                def _():
                    remote.wait()

                @pl.when(jnp.logical_not(away))
                def _():
                    inside.wait()


def local(tokens, tissue, gain1, qkv_w, bias, out_w, gain2, up_w, down_w):
    planes, rows, across, width = tokens.shape
    n_sec = lax.axis_size("sec")
    n_brick = lax.axis_size("brick")
    heads = bias.shape[0]
    hbm = pl.BlockSpec(memory_space=pltpu.HBM)
    vmem = pl.BlockSpec(memory_space=pltpu.VMEM)
    parts = across // WIN
    high = planes * n_brick
    wide = rows // n_brick
    blocks = pl.pallas_call(
        functools.partial(
            block_kernel, head_size=width // heads, n_sec=n_sec, n_brick=n_brick
        ),
        out_shape=jax.ShapeDtypeStruct((parts, high, wide * WIN, width), jnp.bfloat16),
        in_specs=[hbm, vmem, vmem, hbm, hbm, hbm, vmem, hbm, hbm],
        out_specs=hbm,
        scratch_shapes=[
            pltpu.VMEM(tokens.shape, jnp.bfloat16),
            pltpu.VMEM((rows // WIN, parts, planes, SQUARE, width), jnp.bfloat16),
            pltpu.VMEM((WINDOWS, WIN, SQUARE, width), jnp.bfloat16),
            pltpu.VMEM((WINDOWS, WIN, SQUARE, width), jnp.bfloat16),
            pltpu.VMEM(qkv_w.shape, jnp.bfloat16),
            pltpu.VMEM(bias.shape, jnp.bfloat16),
            pltpu.VMEM(out_w.shape, jnp.bfloat16),
            pltpu.VMEM(up_w.shape, jnp.bfloat16),
            pltpu.VMEM(down_w.shape, jnp.bfloat16),
            pltpu.VMEM((TOKENS, 3 * width), jnp.bfloat16),
            pltpu.VMEM((TOKENS, width), jnp.bfloat16),
            pltpu.VMEM((TOKENS, LANES), jnp.bfloat16),
            pltpu.VMEM((TOKENS, LANES), jnp.bfloat16),
            pltpu.VMEM((TOKENS, LANES), jnp.float32),
            pltpu.SemaphoreType.DMA,
            pltpu.SemaphoreType.DMA((5,)),
            pltpu.SemaphoreType.DMA((4, n_brick)),
            pltpu.SemaphoreType.DMA((4, n_brick)),
            pltpu.SemaphoreType.DMA((WINDOWS, 4)),
            pltpu.SemaphoreType.DMA((WINDOWS, 4)),
        ],
        compiler_params=pltpu.CompilerParams(
            collective_id=0, has_side_effects=True, vmem_limit_bytes=56 * 2**20
        ),
    )(tokens, tissue, gain1, qkv_w, bias, out_w, gain2, up_w, down_w)
    blocks = blocks.reshape(parts, high, wide, WIN, width)
    return jnp.concatenate(
        [blocks[1, :, :, WIN - SHIFT :], blocks[0], blocks[1, :, :, : WIN - SHIFT]], axis=2
    )


def solution(mesh):
    placed = (
        P(("sec", "brick"), None, None, None),
        P("sec", "brick", None, None),
        P(),
        P(),
        P(),
        P(),
        P(),
        P(),
        P(),
    )
    return jax.shard_map(
        local, mesh=mesh, in_specs=placed, out_specs=P("sec", "brick", None, None), check_vma=False
    )
```

```python
import functools

import jax
import jax.numpy as jnp
from jax import lax
from jax.experimental import pallas as pl
from jax.experimental.pallas import tpu as pltpu
from jax.sharding import PartitionSpec as P

WIN = 8
SHIFT = 4
EPS = 1e-05
TOKENS = WIN**3
LANES = 128
MASKED = -1e30
ROWS = 256
UNITS = 512
SQUARE = WIN * WIN
WINDOWS = 8
MESH = pl.DeviceIdType.MESH


def layer_norm(values, gain_row):
    centered = values - jnp.mean(values, axis=-1, keepdims=True)
    variance = jnp.mean(centered * centered, axis=-1, keepdims=True)
    return centered * lax.rsqrt(variance + EPS) * gain_row


def gelu(v):
    return 0.5 * v * (1.0 + lax.erf(v * (0.5**0.5)))


def slot(a, b, c):
    return 4 * (1 - b) + 2 * c + 1 - a


def block_kernel(
    tokens,
    tissue_ref,
    gain1_ref,
    qkv_hbm,
    bias_hbm,
    out_w_hbm,
    gain2_ref,
    up_hbm,
    down_hbm,
    out,
    cells,
    stage,
    recv,
    half,
    done,
    qkv_ref,
    bias_ref,
    out_w_ref,
    up_ref,
    down_ref,
    qkv,
    mix,
    key_mask,
    label_hot,
    kept,
    cells_sem,
    weight_sem,
    send_sem,
    recv_sem,
    back_send,
    back_recv,
    *,
    head_size,
    n_sec,
    n_brick,
):
    sec = lax.axis_index("sec")
    me = lax.axis_index("brick")
    planes = tokens.shape[0]
    rows = tokens.shape[1]
    width = tokens.shape[-1]
    early = SHIFT // planes
    depth = planes * n_brick
    rolled = lax.rem(planes * me + depth - SHIFT, depth)
    my_a = lax.div(rolled, WIN)
    my_plane = lax.rem(rolled, WIN)
    is_early = me < early
    to_sec = lax.rem(sec + n_sec - is_early.astype(jnp.int32), n_sec)

    barrier = pltpu.get_barrier_semaphore()

    def greet(s, b):
        pl.semaphore_signal(barrier, inc=1, device_id=(s, b), device_id_type=MESH)

    above = lax.rem(sec + 1, n_sec)
    below = lax.rem(sec + n_sec - 1, n_sec)
    right = lax.rem(me + 1, n_brick)
    left = lax.rem(me + n_brick - 1, n_brick)

    cells_copy = pltpu.make_async_copy(tokens, cells, cells_sem)
    cells_copy.start()

    @pl.loop(0, early)
    def _(k):
        greet(above, k)

    @pl.loop(early, n_brick)
    def _(k):
        @pl.when(k != me)
        def _():
            greet(sec, k)

    greet(sec, left)
    greet(below, me)
    greet(below, left)

    weight_copies = [
        pltpu.make_async_copy(source, target, weight_sem.at[i])
        for i, (source, target) in enumerate(
            (
                (qkv_hbm, qkv_ref),
                (bias_hbm, bias_ref),
                (out_w_hbm, out_w_ref),
                (up_hbm, up_ref),
                (down_hbm, down_ref),
            )
        )
    ]

    cells_copy.wait()

    def store_cut(block, m, p, at, count):
        block = pltpu.roll(block.astype(jnp.float32), 2 * WIN - SHIFT, 1)
        for c in range(2):
            part = block[:, c * WIN : (c + 1) * WIN].reshape(count * WIN, width)
            stage[m, c, p, pl.ds(at, count * WIN)] = part.astype(jnp.bfloat16)

    for p in range(planes):

        @pl.loop(0, rows // WIN - 1)
        def _(m):
            store_cut(cells[p, pl.ds(m * WIN + SHIFT, WIN)], m, p, 0, WIN)

        last = rows // WIN - 1
        store_cut(cells[p, rows - SHIFT :], last, p, 0, SHIFT)
        store_cut(cells[p, :SHIFT], last, p, SHIFT * WIN, SHIFT)

    pl.semaphore_wait(
        barrier, n_brick + 2 + is_early.astype(jnp.int32)
    )

    def piece(j, b, c):
        d = lax.rem(me + j, n_brick)
        source = stage.at[2 * d + b, c]
        target = recv.at[slot(my_a, b, c), pl.ds(my_plane, planes)]
        remote = pltpu.make_async_remote_copy(
            src_ref=source,
            dst_ref=target,
            send_sem=send_sem.at[2 * b + c, j],
            recv_sem=recv_sem.at[2 * b + c, me],
            device_id=(to_sec, d),
            device_id_type=MESH,
        )
        inside = pltpu.make_async_copy(source, target, recv_sem.at[2 * b + c, me])
        return remote, inside

    for b in (1, 0):
        for c in (0, 1):

            @pl.loop(1, n_brick)
            def _(j):
                piece(j, b, c)[0].start()

            remote, inside = piece(0, b, c)

            @pl.when(is_early)
            def _():
                remote.start()

            @pl.when(jnp.logical_not(is_early))
            def _():
                inside.start()

    for copy in weight_copies:
        copy.start()
    for copy in weight_copies:
        copy.wait()

    heads_per_group = LANES // head_size
    groups = width // LANES

    def back(q, ph, rh):
        a = 1 - lax.rem(q, 2)
        b = 1 - lax.div(q, 2)
        z0 = lax.rem(SHIFT + WIN * a + SHIFT * ph, 2 * WIN)
        y0 = lax.rem(SHIFT + WIN * b + SHIFT * rh, 2 * WIN)
        source = done.at[q, pl.ds(SHIFT * ph, SHIFT), pl.ds(SHIFT * rh, SHIFT)]
        target = out.at[pl.ds(z0, SHIFT), pl.ds(y0, SHIFT)]
        away = a * ph + b * rh > 0
        remote = pltpu.make_async_remote_copy(
            src_ref=source,
            dst_ref=target,
            send_sem=back_send.at[q, 2 * ph + rh],
            recv_sem=back_recv.at[q, 2 * ph + rh],
            device_id=(lax.rem(sec + a * ph, n_sec), lax.rem(me + b * rh, n_brick)),
            device_id_type=MESH,
        )
        inside = pltpu.make_async_copy(source, target, back_recv.at[q, 2 * ph + rh])
        return away, remote, inside

    @pl.loop(0, WINDOWS)
    def _(t):
        a = 1 - lax.rem(t, 2)
        c = lax.rem(lax.div(t, 2), 2)
        b = 1 - lax.div(t, 4)

        for i in range(WIN // planes):
            k = lax.rem(early + a * (WIN // planes) + i, n_brick)
            here = recv.at[t, pl.ds(i * planes, planes)]
            pltpu.make_async_copy(here, here, recv_sem.at[2 * b + c, k]).wait()

        @pl.when(t == WINDOWS - 2)
        def _():
            for q in (0, 1):
                for ph in range(2):
                    back(q, ph, 1)[1].start()

        z_last = (sec == n_sec - 1).astype(jnp.int32) * a
        y_last = (me == n_brick - 1).astype(jnp.int32) * b
        token = lax.broadcasted_iota(jnp.int32, (TOKENS, LANES), 0)
        lane = lax.broadcasted_iota(jnp.int32, (TOKENS, LANES), 1)
        fz = ((token // SQUARE) >= SHIFT).astype(jnp.int32) * z_last
        fy = (((token // WIN) % WIN) >= SHIFT).astype(jnp.int32) * y_last
        fx = ((token % WIN) >= SHIFT).astype(jnp.int32) * c
        label = 4 * fz + 2 * fy + fx
        here = label == lane
        marks = tissue_ref[a, b, pl.ds(c, 1), :].astype(jnp.float32)
        marks = jnp.broadcast_to(marks.reshape(1, TOKENS), (LANES, TOKENS)).T
        kept[...] = marks
        label_hot[...] = jnp.where(here, 1.0, 0.0).astype(jnp.bfloat16)
        key_mask[...] = jnp.where(here & (marks > 0.5), 0.0, MASKED).astype(jnp.bfloat16)

        x = recv[t].reshape(TOKENS, width).astype(jnp.float32)
        normed = layer_norm(x, gain1_ref[...].reshape(1, width)).astype(jnp.bfloat16)
        scale = head_size ** (-0.5)
        qkv[:, :width] = (
            jnp.dot(normed, qkv_ref[:, :width], preferred_element_type=jnp.float32) * scale
        ).astype(jnp.bfloat16)
        for part in (1, 2):
            cols = slice(part * width, (part + 1) * width)
            qkv[:, cols] = jnp.dot(
                normed, qkv_ref[:, cols], preferred_element_type=jnp.float32
            ).astype(jnp.bfloat16)

        @pl.loop(0, groups, unroll=True)
        def _(g):
            at = pl.multiple_of(g * LANES, LANES)
            keys = jnp.concatenate(
                [qkv[:, pl.ds(pl.multiple_of(width + at, LANES), LANES)], key_mask[...]],
                axis=1,
            )
            values = jnp.concatenate(
                [
                    qkv[:, pl.ds(pl.multiple_of(2 * width + at, LANES), LANES)],
                    jnp.ones((TOKENS, LANES), jnp.bfloat16),
                ],
                axis=1,
            )
            lane_head = lax.broadcasted_iota(jnp.int32, (ROWS, LANES), 1) // head_size
            for r in range(TOKENS // ROWS):
                span = slice(r * ROWS, (r + 1) * ROWS)
                queries = qkv[span, pl.ds(at, LANES)]
                hot = label_hot[span, :]
                total = None
                for h in range(heads_per_group):
                    mine = lane_head == h
                    query = jnp.where(mine, queries, jnp.zeros_like(queries))
                    scores = lax.dot_general(
                        jnp.concatenate([query, hot], axis=1),
                        keys,
                        (((1,), (1,)), ((), ())),
                        preferred_element_type=jnp.float32,
                    )
                    scores = scores + bias_ref[g * heads_per_group + h, span, :].astype(
                        jnp.float32
                    )
                    top = jnp.max(scores, axis=-1, keepdims=True)
                    raised = jnp.exp(scores - top).astype(jnp.bfloat16)
                    got = jnp.dot(raised, values, preferred_element_type=jnp.float32)
                    value, weight = got[:, :LANES], got[:, LANES:]
                    if total is None:
                        total, sums = value, weight
                    else:
                        total = jnp.where(mine, value, total)
                        sums = jnp.where(mine, weight, sums)
                mix[span, pl.ds(at, LANES)] = (total / sums).astype(jnp.bfloat16)

        x = recv[t].reshape(TOKENS, width).astype(jnp.float32)
        attended = x + jnp.dot(mix[...], out_w_ref[...], preferred_element_type=jnp.float32)
        normed2 = layer_norm(attended, gain2_ref[...].reshape(1, width)).astype(jnp.bfloat16)
        result = attended
        for j in range(up_ref.shape[1] // UNITS):
            units = slice(j * UNITS, (j + 1) * UNITS)
            feed = gelu(
                jnp.dot(normed2, up_ref[:, units], preferred_element_type=jnp.float32)
            ).astype(jnp.bfloat16)
            result = result + jnp.dot(
                feed, down_ref[units, :], preferred_element_type=jnp.float32
            )
        keep = jnp.concatenate([kept[...]] * groups, axis=1) > 0.5
        half[a, c] = jnp.where(keep, result, x).astype(jnp.bfloat16)

        @pl.when(c == 1)
        def _():
            q = 2 * (1 - b) + 1 - a
            both = jnp.concatenate(
                [
                    half[a, i].astype(jnp.float32).reshape(SQUARE, WIN, width)
                    for i in range(2)
                ],
                axis=1,
            )
            both = pltpu.roll(both, SHIFT, 1).astype(jnp.bfloat16)
            done[q] = both.reshape(WIN, WIN, 2 * WIN, width)
            for ph in range(2):
                for rh in range(2):
                    away, remote, inside = back(q, ph, rh)

                    @pl.when(jnp.logical_and(away, b * rh == 0))
                    def _():
                        remote.start()

                    @pl.when(jnp.logical_not(away))
                    def _():
                        inside.start()

    for b in (1, 0):
        for c in (0, 1):

            @pl.loop(1, n_brick)
            def _(j):
                piece(j, b, c)[0].wait_send()

            remote, _ = piece(0, b, c)

            @pl.when(is_early)
            def _():
                remote.wait_send()

    @pl.loop(0, WINDOWS // 2)
    def _(q):
        for ph in range(2):
            for rh in range(2):
                away, remote, inside = back(q, ph, rh)

                @pl.when(away)
                def _():
                    remote.wait()

                @pl.when(jnp.logical_not(away))
                def _():
                    inside.wait()


def local(tokens, tissue, gain1, qkv_w, bias, out_w, gain2, up_w, down_w):
    planes, rows, across, width = tokens.shape
    n_sec = lax.axis_size("sec")
    n_brick = lax.axis_size("brick")
    heads = bias.shape[0]
    hbm = pl.BlockSpec(memory_space=pltpu.HBM)
    vmem = pl.BlockSpec(memory_space=pltpu.VMEM)
    parts = across // WIN
    high = planes * n_brick
    wide = rows // n_brick
    return pl.pallas_call(
        functools.partial(
            block_kernel, head_size=width // heads, n_sec=n_sec, n_brick=n_brick
        ),
        out_shape=pltpu.VMEM((high, wide, across, width), jnp.bfloat16),
        in_specs=[hbm, vmem, vmem, hbm, hbm, hbm, vmem, hbm, hbm],
        out_specs=pl.BlockSpec(memory_space=pltpu.VMEM),
        scratch_shapes=[
            pltpu.VMEM(tokens.shape, jnp.bfloat16),
            pltpu.VMEM((rows // WIN, parts, planes, SQUARE, width), jnp.bfloat16),
            pltpu.VMEM((WINDOWS, WIN, SQUARE, width), jnp.bfloat16),
            pltpu.VMEM((2, 2, TOKENS, width), jnp.bfloat16),
            pltpu.VMEM((WINDOWS // 2, WIN, WIN, across, width), jnp.bfloat16),
            pltpu.VMEM(qkv_w.shape, jnp.bfloat16),
            pltpu.VMEM(bias.shape, jnp.bfloat16),
            pltpu.VMEM(out_w.shape, jnp.bfloat16),
            pltpu.VMEM(up_w.shape, jnp.bfloat16),
            pltpu.VMEM(down_w.shape, jnp.bfloat16),
            pltpu.VMEM((TOKENS, 3 * width), jnp.bfloat16),
            pltpu.VMEM((TOKENS, width), jnp.bfloat16),
            pltpu.VMEM((TOKENS, LANES), jnp.bfloat16),
            pltpu.VMEM((TOKENS, LANES), jnp.bfloat16),
            pltpu.VMEM((TOKENS, LANES), jnp.float32),
            pltpu.SemaphoreType.DMA,
            pltpu.SemaphoreType.DMA((5,)),
            pltpu.SemaphoreType.DMA((4, n_brick)),
            pltpu.SemaphoreType.DMA((4, n_brick)),
            pltpu.SemaphoreType.DMA((WINDOWS // 2, 4)),
            pltpu.SemaphoreType.DMA((WINDOWS // 2, 4)),
        ],
        compiler_params=pltpu.CompilerParams(
            collective_id=0, has_side_effects=True, vmem_limit_bytes=58 * 2**20
        ),
    )(tokens, tissue, gain1, qkv_w, bias, out_w, gain2, up_w, down_w)


def solution(mesh):
    placed = (
        P(("sec", "brick"), None, None, None),
        P("sec", "brick", None, None),
        P(),
        P(),
        P(),
        P(),
        P(),
        P(),
        P(),
    )
    return jax.shard_map(
        local, mesh=mesh, in_specs=placed, out_specs=P("sec", "brick", None, None), check_vma=False
    )
```

```python
import functools

import jax
import jax.numpy as jnp
from jax import lax
from jax.experimental import pallas as pl
from jax.experimental.pallas import tpu as pltpu
from jax.sharding import PartitionSpec as P

WIN = 8
SHIFT = 4
EPS = 1e-05
TOKENS = WIN**3
LANES = 128
MASKED = -1e30
ROWS = 256
UNITS = 512
SQUARE = WIN * WIN
WINDOWS = 8
MESH = pl.DeviceIdType.MESH


def layer_norm(values, gain_row):
    centered = values - jnp.mean(values, axis=-1, keepdims=True)
    variance = jnp.mean(centered * centered, axis=-1, keepdims=True)
    return centered * lax.rsqrt(variance + EPS) * gain_row


def gelu(v):
    return 0.5 * v * (1.0 + lax.erf(v * (0.5**0.5)))


def slot(a, b, c):
    return 4 * (1 - b) + 2 * c + 1 - a


def block_kernel(
    tokens,
    tissue_ref,
    gain1_ref,
    qkv_hbm,
    bias_hbm,
    out_w_hbm,
    gain2_ref,
    up_hbm,
    down_hbm,
    out,
    cells,
    stage,
    recv,
    half,
    done,
    relay,
    qkv_ref,
    bias_ref,
    out_w_ref,
    up_ref,
    down_ref,
    qkv,
    mix,
    key_mask,
    label_hot,
    kept,
    cells_sem,
    weight_sem,
    send_sem,
    recv_sem,
    back_send,
    back_recv,
    relay_sem,
    *,
    head_size,
    n_sec,
    n_brick,
    relayed,
):
    sec = lax.axis_index("sec")
    me = lax.axis_index("brick")
    planes = tokens.shape[0]
    rows = tokens.shape[1]
    width = tokens.shape[-1]
    early = SHIFT // planes
    depth = planes * n_brick
    rolled = lax.rem(planes * me + depth - SHIFT, depth)
    my_a = lax.div(rolled, WIN)
    my_plane = lax.rem(rolled, WIN)
    is_early = me < early
    to_sec = lax.rem(sec + n_sec - is_early.astype(jnp.int32), n_sec)

    barrier = pltpu.get_barrier_semaphore()

    def greet(s, b):
        pl.semaphore_signal(barrier, inc=1, device_id=(s, b), device_id_type=MESH)

    above = lax.rem(sec + 1, n_sec)
    below = lax.rem(sec + n_sec - 1, n_sec)
    right = lax.rem(me + 1, n_brick)
    left = lax.rem(me + n_brick - 1, n_brick)

    cells_copy = pltpu.make_async_copy(tokens, cells, cells_sem)
    cells_copy.start()

    @pl.loop(0, early)
    def _(k):
        greet(above, k)

    @pl.loop(early, n_brick)
    def _(k):
        @pl.when(k != me)
        def _():
            greet(sec, k)

    greet(sec, left)
    greet(below, me)
    greet(below, left)
    greet(below, lax.rem(me + n_brick - 2, n_brick))

    weight_copies = [
        pltpu.make_async_copy(source, target, weight_sem.at[i])
        for i, (source, target) in enumerate(
            (
                (qkv_hbm, qkv_ref),
                (bias_hbm, bias_ref),
                (out_w_hbm, out_w_ref),
                (up_hbm, up_ref),
                (down_hbm, down_ref),
            )
        )
    ]

    cells_copy.wait()

    def store_cut(block, m, p, at, count):
        block = pltpu.roll(block.astype(jnp.float32), 2 * WIN - SHIFT, 1)
        for c in range(2):
            part = block[:, c * WIN : (c + 1) * WIN].reshape(count * WIN, width)
            stage[m, c, p, pl.ds(at, count * WIN)] = part.astype(jnp.bfloat16)

    for p in range(planes):

        @pl.loop(0, rows // WIN - 1)
        def _(m):
            store_cut(cells[p, pl.ds(m * WIN + SHIFT, WIN)], m, p, 0, WIN)

        last = rows // WIN - 1
        store_cut(cells[p, rows - SHIFT :], last, p, 0, SHIFT)
        store_cut(cells[p, :SHIFT], last, p, SHIFT * WIN, SHIFT)

    pl.semaphore_wait(
        barrier, n_brick + 3 + is_early.astype(jnp.int32)
    )

    def piece(j, b, c):
        d = lax.rem(me + j, n_brick)
        source = stage.at[2 * d + b, c]
        target = recv.at[slot(my_a, b, c), pl.ds(my_plane, planes)]
        remote = pltpu.make_async_remote_copy(
            src_ref=source,
            dst_ref=target,
            send_sem=send_sem.at[2 * b + c, j],
            recv_sem=recv_sem.at[2 * b + c, me],
            device_id=(to_sec, d),
            device_id_type=MESH,
        )
        inside = pltpu.make_async_copy(source, target, recv_sem.at[2 * b + c, me])
        return remote, inside

    def send(b, c):
        @pl.loop(1, n_brick)
        def _(j):
            piece(j, b, c)[0].start()

        remote, inside = piece(0, b, c)

        @pl.when(is_early)
        def _():
            remote.start()

        @pl.when(jnp.logical_not(is_early))
        def _():
            inside.start()

    send(1, 0)

    for copy in weight_copies:
        copy.start()
    for copy in weight_copies:
        copy.wait()

    half_way = n_brick // 2
    crossing = jnp.logical_and(relayed, lax.rem(me, half_way) == half_way - 1)
    carrying = jnp.logical_and(relayed, lax.rem(me, half_way) == half_way - 2)
    heads_per_group = LANES // head_size
    groups = width // LANES

    def back(q, ph, rh):
        a = 1 - lax.rem(q, 2)
        b = 1 - lax.div(q, 2)
        z0 = lax.rem(SHIFT + WIN * a + SHIFT * ph, 2 * WIN)
        y0 = lax.rem(SHIFT + WIN * b + SHIFT * rh, 2 * WIN)
        source = done.at[q, pl.ds(SHIFT * ph, SHIFT), pl.ds(SHIFT * rh, SHIFT)]
        target = out.at[pl.ds(z0, SHIFT), pl.ds(y0, SHIFT)]
        away = a * ph + b * rh > 0
        direct = jnp.logical_not(
            jnp.logical_and(jnp.logical_and(q == 0, rh == 1), crossing)
        )
        remote = pltpu.make_async_remote_copy(
            src_ref=source,
            dst_ref=target,
            send_sem=back_send.at[q, 2 * ph + rh],
            recv_sem=back_recv.at[q, 2 * ph + rh],
            device_id=(lax.rem(sec + a * ph, n_sec), lax.rem(me + b * rh, n_brick)),
            device_id_type=MESH,
        )
        inside = pltpu.make_async_copy(source, target, back_recv.at[q, 2 * ph + rh])
        return away, direct, remote, inside

    def hand_over():
        return pltpu.make_async_remote_copy(
            src_ref=done.at[0, :, pl.ds(SHIFT, SHIFT)],
            dst_ref=relay,
            send_sem=relay_sem.at[0],
            recv_sem=relay_sem.at[1],
            device_id=(sec, lax.rem(me + n_brick - 1, n_brick)),
            device_id_type=MESH,
        )

    def pass_on(ph):
        return pltpu.make_async_remote_copy(
            src_ref=relay.at[pl.ds(SHIFT * ph, SHIFT)],
            dst_ref=out.at[pl.ds((WIN + SHIFT) * (1 - ph), SHIFT), pl.ds(0, SHIFT)],
            send_sem=relay_sem.at[2 + ph],
            recv_sem=back_recv.at[0, 2 * ph + 1],
            device_id=(lax.rem(sec + ph, n_sec), lax.rem(me + 2, n_brick)),
            device_id_type=MESH,
        )

    @pl.loop(0, WINDOWS)
    def _(t):
        a = 1 - lax.rem(t, 2)
        c = lax.rem(lax.div(t, 2), 2)
        b = 1 - lax.div(t, 4)

        @pl.when(jnp.logical_or(t == 2, t == 4))
        def _():
            send(0, lax.div(t, 2) - 1)

        for i in range(WIN // planes):
            k = lax.rem(early + a * (WIN // planes) + i, n_brick)
            here = recv.at[t, pl.ds(i * planes, planes)]
            pltpu.make_async_copy(here, here, recv_sem.at[2 * b + c, k]).wait()

            if i == WIN // planes // 2 - 1:
                @pl.when(t == 0)
                def _():
                    send(1, 1)

        @pl.when(t == WINDOWS - 2)
        def _():
            for ph in range(2):
                back(1, ph, 1)[2].start()
            for ph in range(2):
                _, direct, remote, _ = back(0, ph, 1)

                @pl.when(direct)
                def _():
                    remote.start()


        if relayed:

            @pl.when(jnp.logical_and(carrying, t == WINDOWS - 2))
            def _():
                hand_over().wait_recv()
                for ph in range(2):
                    pass_on(ph).start()

        z_last = (sec == n_sec - 1).astype(jnp.int32) * a
        y_last = (me == n_brick - 1).astype(jnp.int32) * b
        token = lax.broadcasted_iota(jnp.int32, (TOKENS, LANES), 0)
        lane = lax.broadcasted_iota(jnp.int32, (TOKENS, LANES), 1)
        fz = ((token // SQUARE) >= SHIFT).astype(jnp.int32) * z_last
        fy = (((token // WIN) % WIN) >= SHIFT).astype(jnp.int32) * y_last
        fx = ((token % WIN) >= SHIFT).astype(jnp.int32) * c
        label = 4 * fz + 2 * fy + fx
        here = label == lane
        marks = tissue_ref[a, b, pl.ds(c, 1), :].astype(jnp.float32)
        marks = jnp.broadcast_to(marks.reshape(1, TOKENS), (LANES, TOKENS)).T
        kept[...] = marks
        label_hot[...] = jnp.where(here, 1.0, 0.0).astype(jnp.bfloat16)
        key_mask[...] = jnp.where(here & (marks > 0.5), 0.0, MASKED).astype(jnp.bfloat16)

        x = recv[t].reshape(TOKENS, width).astype(jnp.float32)
        normed = layer_norm(x, gain1_ref[...].reshape(1, width)).astype(jnp.bfloat16)
        scale = head_size ** (-0.5)
        qkv[:, :width] = (
            jnp.dot(normed, qkv_ref[:, :width], preferred_element_type=jnp.float32) * scale
        ).astype(jnp.bfloat16)
        for part in (1, 2):
            cols = slice(part * width, (part + 1) * width)
            qkv[:, cols] = jnp.dot(
                normed, qkv_ref[:, cols], preferred_element_type=jnp.float32
            ).astype(jnp.bfloat16)

        @pl.loop(0, groups, unroll=True)
        def _(g):
            at = pl.multiple_of(g * LANES, LANES)
            keys = jnp.concatenate(
                [qkv[:, pl.ds(pl.multiple_of(width + at, LANES), LANES)], key_mask[...]],
                axis=1,
            )
            values = jnp.concatenate(
                [
                    qkv[:, pl.ds(pl.multiple_of(2 * width + at, LANES), LANES)],
                    jnp.ones((TOKENS, LANES), jnp.bfloat16),
                ],
                axis=1,
            )
            lane_head = lax.broadcasted_iota(jnp.int32, (ROWS, LANES), 1) // head_size
            for r in range(TOKENS // ROWS):
                span = slice(r * ROWS, (r + 1) * ROWS)
                queries = qkv[span, pl.ds(at, LANES)]
                hot = label_hot[span, :]
                total = None
                for h in range(heads_per_group):
                    mine = lane_head == h
                    query = jnp.where(mine, queries, jnp.zeros_like(queries))
                    scores = lax.dot_general(
                        jnp.concatenate([query, hot], axis=1),
                        keys,
                        (((1,), (1,)), ((), ())),
                        preferred_element_type=jnp.float32,
                    )
                    scores = scores + bias_ref[g * heads_per_group + h, span, :].astype(
                        jnp.float32
                    )
                    top = jnp.max(scores, axis=-1, keepdims=True)
                    raised = jnp.exp(scores - top).astype(jnp.bfloat16)
                    got = jnp.dot(raised, values, preferred_element_type=jnp.float32)
                    value, weight = got[:, :LANES], got[:, LANES:]
                    if total is None:
                        total, sums = value, weight
                    else:
                        total = jnp.where(mine, value, total)
                        sums = jnp.where(mine, weight, sums)
                mix[span, pl.ds(at, LANES)] = (total / sums).astype(jnp.bfloat16)

        x = recv[t].reshape(TOKENS, width).astype(jnp.float32)
        attended = x + jnp.dot(mix[...], out_w_ref[...], preferred_element_type=jnp.float32)
        normed2 = layer_norm(attended, gain2_ref[...].reshape(1, width)).astype(jnp.bfloat16)
        result = attended
        for j in range(up_ref.shape[1] // UNITS):
            units = slice(j * UNITS, (j + 1) * UNITS)
            feed = gelu(
                jnp.dot(normed2, up_ref[:, units], preferred_element_type=jnp.float32)
            ).astype(jnp.bfloat16)
            result = result + jnp.dot(
                feed, down_ref[units, :], preferred_element_type=jnp.float32
            )
        keep = jnp.concatenate([kept[...]] * groups, axis=1) > 0.5
        half[a, c] = jnp.where(keep, result, x).astype(jnp.bfloat16)

        @pl.when(c == 1)
        def _():
            q = 2 * (1 - b) + 1 - a
            both = jnp.concatenate(
                [
                    half[a, i].astype(jnp.float32).reshape(SQUARE, WIN, width)
                    for i in range(2)
                ],
                axis=1,
            )
            both = pltpu.roll(both, SHIFT, 1).astype(jnp.bfloat16)
            done[q] = both.reshape(WIN, WIN, 2 * WIN, width)
            for ph in range(2):
                for rh in range(2):
                    away, direct, remote, inside = back(q, ph, rh)

                    @pl.when(jnp.logical_and(away, b * rh == 0))
                    def _():
                        remote.start()

                    @pl.when(jnp.logical_not(away))
                    def _():
                        inside.start()

            if relayed:

                @pl.when(jnp.logical_and(crossing, q == 0))
                def _():
                    hand_over().start()

    for b in (1, 0):
        for c in (0, 1):

            @pl.loop(1, n_brick)
            def _(j):
                piece(j, b, c)[0].wait_send()

            remote, _ = piece(0, b, c)

            @pl.when(is_early)
            def _():
                remote.wait_send()

    @pl.loop(0, WINDOWS // 2)
    def _(q):
        for ph in range(2):
            for rh in range(2):
                away, direct, remote, inside = back(q, ph, rh)

                @pl.when(away)
                def _():
                    remote.wait_recv()

                @pl.when(jnp.logical_and(away, direct))
                def _():
                    remote.wait_send()

                @pl.when(jnp.logical_not(away))
                def _():
                    inside.wait()

    if relayed:

        @pl.when(crossing)
        def _():
            hand_over().wait_send()

        @pl.when(carrying)
        def _():
            for ph in range(2):
                pass_on(ph).wait_send()


def local(tokens, tissue, gain1, qkv_w, bias, out_w, gain2, up_w, down_w):
    planes, rows, across, width = tokens.shape
    n_sec = lax.axis_size("sec")
    n_brick = lax.axis_size("brick")
    heads = bias.shape[0]
    hbm = pl.BlockSpec(memory_space=pltpu.HBM)
    vmem = pl.BlockSpec(memory_space=pltpu.VMEM)
    parts = across // WIN
    high = planes * n_brick
    wide = rows // n_brick
    return pl.pallas_call(
        functools.partial(
            block_kernel,
            head_size=width // heads,
            n_sec=n_sec,
            n_brick=n_brick,
            relayed=n_brick == 8,
        ),
        out_shape=pltpu.VMEM((high, wide, across, width), jnp.bfloat16),
        in_specs=[hbm, vmem, vmem, hbm, hbm, hbm, vmem, hbm, hbm],
        out_specs=pl.BlockSpec(memory_space=pltpu.VMEM),
        scratch_shapes=[
            pltpu.VMEM(tokens.shape, jnp.bfloat16),
            pltpu.VMEM((rows // WIN, parts, planes, SQUARE, width), jnp.bfloat16),
            pltpu.VMEM((WINDOWS, WIN, SQUARE, width), jnp.bfloat16),
            pltpu.VMEM((2, 2, TOKENS, width), jnp.bfloat16),
            pltpu.VMEM((WINDOWS // 2, WIN, WIN, across, width), jnp.bfloat16),
            pltpu.VMEM((WIN, SHIFT, across, width), jnp.bfloat16),
            pltpu.VMEM(qkv_w.shape, jnp.bfloat16),
            pltpu.VMEM(bias.shape, jnp.bfloat16),
            pltpu.VMEM(out_w.shape, jnp.bfloat16),
            pltpu.VMEM(up_w.shape, jnp.bfloat16),
            pltpu.VMEM(down_w.shape, jnp.bfloat16),
            pltpu.VMEM((TOKENS, 3 * width), jnp.bfloat16),
            pltpu.VMEM((TOKENS, width), jnp.bfloat16),
            pltpu.VMEM((TOKENS, LANES), jnp.bfloat16),
            pltpu.VMEM((TOKENS, LANES), jnp.bfloat16),
            pltpu.VMEM((TOKENS, LANES), jnp.float32),
            pltpu.SemaphoreType.DMA,
            pltpu.SemaphoreType.DMA((5,)),
            pltpu.SemaphoreType.DMA((4, n_brick)),
            pltpu.SemaphoreType.DMA((4, n_brick)),
            pltpu.SemaphoreType.DMA((WINDOWS // 2, 4)),
            pltpu.SemaphoreType.DMA((WINDOWS // 2, 4)),
            pltpu.SemaphoreType.DMA((4,)),
        ],
        compiler_params=pltpu.CompilerParams(
            collective_id=0, has_side_effects=True, vmem_limit_bytes=58 * 2**20
        ),
    )(tokens, tissue, gain1, qkv_w, bias, out_w, gain2, up_w, down_w)


def solution(mesh):
    placed = (
        P(("sec", "brick"), None, None, None),
        P("sec", "brick", None, None),
        P(),
        P(),
        P(),
        P(),
        P(),
        P(),
        P(),
    )
    return jax.shard_map(
        local, mesh=mesh, in_specs=placed, out_specs=P("sec", "brick", None, None), check_vma=False
    )
```

```python
import functools

import jax
import jax.numpy as jnp
from jax import lax
from jax.experimental import pallas as pl
from jax.experimental.pallas import tpu as pltpu
from jax.sharding import PartitionSpec as P

WIN = 8
SHIFT = 4
EPS = 1e-05
TOKENS = WIN**3
LANES = 128
MASKED = -1e30
ROWS = 256
HALF = TOKENS // 2
UNITS = 512
SQUARE = WIN * WIN
WINDOWS = 8
MESH = pl.DeviceIdType.MESH


def layer_norm(values, gain_row):
    centered = values - jnp.mean(values, axis=-1, keepdims=True)
    variance = jnp.mean(centered * centered, axis=-1, keepdims=True)
    return centered * lax.rsqrt(variance + EPS) * gain_row


def gelu(v):
    return 0.5 * v * (1.0 + lax.erf(v * (0.5**0.5)))


def slot(a, b, c):
    return 4 * (1 - b) + 2 * c + 1 - a


def block_kernel(
    tokens,
    tissue_ref,
    gain1_ref,
    qkv_hbm,
    bias_hbm,
    out_w_hbm,
    gain2_ref,
    up_hbm,
    down_hbm,
    out,
    cells,
    stage,
    recv,
    half,
    done,
    relay,
    qkv_ref,
    bias_ref,
    split_bias,
    gather,
    scatter,
    marked,
    window,
    out_w_ref,
    up_ref,
    down_ref,
    qkv,
    mix,
    key_mask,
    label_hot,
    kept,
    cells_sem,
    weight_sem,
    send_sem,
    recv_sem,
    back_send,
    back_recv,
    relay_sem,
    *,
    head_size,
    n_sec,
    n_brick,
    relayed,
):
    sec = lax.axis_index("sec")
    me = lax.axis_index("brick")
    planes = tokens.shape[0]
    rows = tokens.shape[1]
    width = tokens.shape[-1]
    early = SHIFT // planes
    depth = planes * n_brick
    rolled = lax.rem(planes * me + depth - SHIFT, depth)
    my_a = lax.div(rolled, WIN)
    my_plane = lax.rem(rolled, WIN)
    is_early = me < early
    to_sec = lax.rem(sec + n_sec - is_early.astype(jnp.int32), n_sec)

    barrier = pltpu.get_barrier_semaphore()

    def greet(s, b):
        pl.semaphore_signal(barrier, inc=1, device_id=(s, b), device_id_type=MESH)

    above = lax.rem(sec + 1, n_sec)
    below = lax.rem(sec + n_sec - 1, n_sec)
    right = lax.rem(me + 1, n_brick)
    left = lax.rem(me + n_brick - 1, n_brick)

    cells_copy = pltpu.make_async_copy(tokens, cells, cells_sem)
    cells_copy.start()

    @pl.loop(0, early)
    def _(k):
        greet(above, k)

    @pl.loop(early, n_brick)
    def _(k):
        @pl.when(k != me)
        def _():
            greet(sec, k)

    greet(sec, left)
    greet(below, me)
    greet(below, left)
    greet(below, lax.rem(me + n_brick - 2, n_brick))

    weight_copies = [
        pltpu.make_async_copy(source, target, weight_sem.at[i])
        for i, (source, target) in enumerate(
            (
                (qkv_hbm, qkv_ref),
                (bias_hbm, bias_ref),
                (out_w_hbm, out_w_ref),
                (up_hbm, up_ref),
                (down_hbm, down_ref),
            )
        )
    ]

    cells_copy.wait()

    def store_cut(block, m, p, at, count):
        block = pltpu.roll(block.astype(jnp.float32), 2 * WIN - SHIFT, 1)
        for c in range(2):
            part = block[:, c * WIN : (c + 1) * WIN].reshape(count * WIN, width)
            stage[m, c, p, pl.ds(at, count * WIN)] = part.astype(jnp.bfloat16)

    for p in range(planes):

        @pl.loop(0, rows // WIN - 1)
        def _(m):
            store_cut(cells[p, pl.ds(m * WIN + SHIFT, WIN)], m, p, 0, WIN)

        last = rows // WIN - 1
        store_cut(cells[p, rows - SHIFT :], last, p, 0, SHIFT)
        store_cut(cells[p, :SHIFT], last, p, SHIFT * WIN, SHIFT)

    pl.semaphore_wait(
        barrier, n_brick + 3 + is_early.astype(jnp.int32)
    )

    def piece(j, b, c):
        step = lax.div(j, 2) * (1 - 2 * lax.rem(j + 1, 2))
        d = lax.rem(me + step + n_brick // 2 * jnp.minimum(j, 1) + n_brick, n_brick)
        source = stage.at[2 * d + b, c]
        target = recv.at[slot(my_a, b, c), pl.ds(my_plane, planes)]
        remote = pltpu.make_async_remote_copy(
            src_ref=source,
            dst_ref=target,
            send_sem=send_sem.at[2 * b + c, j],
            recv_sem=recv_sem.at[2 * b + c, me],
            device_id=(to_sec, d),
            device_id_type=MESH,
        )
        inside = pltpu.make_async_copy(source, target, recv_sem.at[2 * b + c, me])
        return remote, inside

    def send(b, c):
        @pl.loop(1, n_brick)
        def _(j):
            piece(j, b, c)[0].start()

        remote, inside = piece(0, b, c)

        @pl.when(is_early)
        def _():
            remote.start()

        @pl.when(jnp.logical_not(is_early))
        def _():
            inside.start()

    send(1, 0)

    for copy in weight_copies:
        copy.start()

    shape = (TOKENS, TOKENS)
    down = lax.broadcasted_iota(jnp.int32, shape, 0)
    right_of = lax.broadcasted_iota(jnp.int32, shape, 1)

    def from_place(p):
        return (p // SHIFT % SQUARE) * WIN + p // HALF * SHIFT + p % SHIFT

    gather[...] = jnp.where(from_place(down) == right_of, 1.0, 0.0).astype(jnp.bfloat16)
    scatter[...] = jnp.where(from_place(right_of) == down, 1.0, 0.0).astype(jnp.bfloat16)
    marks = jnp.concatenate(
        [tissue_ref[i, j].astype(jnp.float32) for i in range(2) for j in range(2)], axis=0
    )
    marked[0] = marks
    marked[1] = jnp.dot(
        marks.astype(jnp.bfloat16), scatter[...], preferred_element_type=jnp.float32
    )

    for copy in weight_copies:
        copy.wait()

    @pl.loop(0, bias_ref.shape[0])
    def _(h):
        moved = jnp.dot(
            bias_ref[h], scatter[...], preferred_element_type=jnp.float32
        ).astype(jnp.bfloat16)
        for r in range(2):
            span = slice(r * HALF, (r + 1) * HALF)
            split_bias[h, r] = jnp.dot(
                gather[span, :], moved[:, span], preferred_element_type=jnp.float32
            ).astype(jnp.bfloat16)

    half_way = n_brick // 2
    crossing = jnp.logical_and(relayed, lax.rem(me, half_way) == half_way - 1)
    carrying = jnp.logical_and(relayed, lax.rem(me, half_way) == half_way - 2)
    heads_per_group = LANES // head_size
    groups = width // LANES

    def back(q, ph, rh):
        a = 1 - lax.rem(q, 2)
        b = 1 - lax.div(q, 2)
        z0 = lax.rem(SHIFT + WIN * a + SHIFT * ph, 2 * WIN)
        y0 = lax.rem(SHIFT + WIN * b + SHIFT * rh, 2 * WIN)
        source = done.at[q, pl.ds(SHIFT * ph, SHIFT), pl.ds(SHIFT * rh, SHIFT)]
        target = out.at[pl.ds(z0, SHIFT), pl.ds(y0, SHIFT)]
        away = a * ph + b * rh > 0
        direct = jnp.logical_not(
            jnp.logical_and(jnp.logical_and(q == 0, rh == 1), crossing)
        )
        remote = pltpu.make_async_remote_copy(
            src_ref=source,
            dst_ref=target,
            send_sem=back_send.at[q, 2 * ph + rh],
            recv_sem=back_recv.at[q, 2 * ph + rh],
            device_id=(lax.rem(sec + a * ph, n_sec), lax.rem(me + b * rh, n_brick)),
            device_id_type=MESH,
        )
        inside = pltpu.make_async_copy(source, target, back_recv.at[q, 2 * ph + rh])
        return away, direct, remote, inside

    def hand_over():
        return pltpu.make_async_remote_copy(
            src_ref=done.at[0, :, pl.ds(SHIFT, SHIFT)],
            dst_ref=relay,
            send_sem=relay_sem.at[0],
            recv_sem=relay_sem.at[1],
            device_id=(sec, lax.rem(me + n_brick - 1, n_brick)),
            device_id_type=MESH,
        )

    def pass_on(ph):
        return pltpu.make_async_remote_copy(
            src_ref=relay.at[pl.ds(SHIFT * ph, SHIFT)],
            dst_ref=out.at[pl.ds((WIN + SHIFT) * (1 - ph), SHIFT), pl.ds(0, SHIFT)],
            send_sem=relay_sem.at[2 + ph],
            recv_sem=back_recv.at[0, 2 * ph + 1],
            device_id=(lax.rem(sec + ph, n_sec), lax.rem(me + 2, n_brick)),
            device_id_type=MESH,
        )

    @pl.loop(0, WINDOWS)
    def _(t):
        a = 1 - lax.rem(t, 2)
        c = lax.rem(lax.div(t, 2), 2)
        b = 1 - lax.div(t, 4)

        @pl.when(jnp.logical_or(t == 1, t == 4))
        def _():
            send(0, lax.div(t, 4))

        for i in range(WIN // planes):
            k = lax.rem(early + a * (WIN // planes) + i, n_brick)
            here = recv.at[t, pl.ds(i * planes, planes)]
            pltpu.make_async_copy(here, here, recv_sem.at[2 * b + c, k]).wait()

            if i == WIN // planes // 2 - 1:
                @pl.when(t == 0)
                def _():
                    send(1, 1)

        @pl.when(t == WINDOWS - 2 + crossing.astype(jnp.int32))
        def _():
            for ph in range(2):
                back(1, ph, 1)[2].start()
            for ph in range(2):
                _, direct, remote, _ = back(0, ph, 1)

                @pl.when(direct)
                def _():
                    remote.start()


        if relayed:

            @pl.when(jnp.logical_and(carrying, t == WINDOWS - 1))
            def _():
                hand_over().wait_recv()
                for ph in range(2):
                    pass_on(ph).start()

        z_last = (sec == n_sec - 1).astype(jnp.int32) * a
        y_last = (me == n_brick - 1).astype(jnp.int32) * b
        token = lax.broadcasted_iota(jnp.int32, (TOKENS, LANES), 0)
        lane = lax.broadcasted_iota(jnp.int32, (TOKENS, LANES), 1)
        square = jnp.where(c == 1, token // SHIFT % SQUARE, token // WIN)
        fz = ((square // WIN) >= SHIFT).astype(jnp.int32) * z_last
        fy = ((square % WIN) >= SHIFT).astype(jnp.int32) * y_last
        label = 2 * fz + fy
        here = label == lane
        marks = marked[c, pl.ds(4 * a + 2 * b + c, 1), :]
        marks = jnp.broadcast_to(marks.reshape(1, TOKENS), (LANES, TOKENS)).T
        kept[...] = marks
        label_hot[...] = jnp.where(here, 1.0, 0.0).astype(jnp.bfloat16)
        key_mask[...] = jnp.where(here & (marks > 0.5), 0.0, MASKED).astype(jnp.bfloat16)

        @pl.when(c == 0)
        def _():
            window[...] = recv[t].reshape(TOKENS, width).astype(jnp.float32)

        @pl.when(c == 1)
        def _():
            window[...] = jnp.dot(
                gather[...], recv[t].reshape(TOKENS, width), preferred_element_type=jnp.float32
            )

        x = window[...]
        normed = layer_norm(x, gain1_ref[...].reshape(1, width)).astype(jnp.bfloat16)
        scale = head_size ** (-0.5)
        qkv[:, :width] = (
            jnp.dot(normed, qkv_ref[:, :width], preferred_element_type=jnp.float32) * scale
        ).astype(jnp.bfloat16)
        for part in (1, 2):
            cols = slice(part * width, (part + 1) * width)
            qkv[:, cols] = jnp.dot(
                normed, qkv_ref[:, cols], preferred_element_type=jnp.float32
            ).astype(jnp.bfloat16)

        def stacked(g, keys_at):
            at = g * LANES
            values = qkv[keys_at, 2 * width + at : 2 * width + at + LANES]
            lane_head = lax.broadcasted_iota(jnp.int32, values.shape, 1) // head_size
            zeros = jnp.zeros_like(values)
            parts = []
            for h in range(heads_per_group):
                mine = lane_head == h
                parts.append(
                    jnp.concatenate(
                        [jnp.where(mine, values, zeros), jnp.where(mine, zeros + 1, zeros)],
                        axis=1,
                    )
                )
            return jnp.concatenate(parts, axis=0)

        def attend(g, r, keys_at, values, bias_of):
            at = g * LANES
            span = slice(r * ROWS, (r + 1) * ROWS)
            keys = jnp.concatenate(
                [qkv[keys_at, width + at : width + at + LANES], key_mask[keys_at, :]], axis=1
            )
            lane_head = lax.broadcasted_iota(jnp.int32, (ROWS, LANES), 1) // head_size
            queries = qkv[span, at : at + LANES]
            hot = label_hot[span, :]
            weights = []
            for h in range(heads_per_group):
                mine = lane_head == h
                query = jnp.where(mine, queries, jnp.zeros_like(queries))
                scores = lax.dot_general(
                    jnp.concatenate([query, hot], axis=1),
                    keys,
                    (((1,), (1,)), ((), ())),
                    preferred_element_type=jnp.float32,
                )
                scores = scores + bias_of(g * heads_per_group + h, r).astype(jnp.float32)
                top = jnp.max(scores, axis=-1, keepdims=True)
                weights.append(jnp.exp(scores - top).astype(jnp.bfloat16))
            got = jnp.dot(
                jnp.concatenate(weights, axis=1), values, preferred_element_type=jnp.float32
            )
            mix[span, at : at + LANES] = (got[:, :LANES] / got[:, LANES:]).astype(jnp.bfloat16)

        @pl.when(c == 0)
        def _():
            for g in range(groups):
                values = stacked(g, slice(0, TOKENS))
                for r in range(TOKENS // ROWS):
                    attend(
                        g,
                        r,
                        slice(0, TOKENS),
                        values,
                        lambda h, r: bias_ref[h, r * ROWS : (r + 1) * ROWS, :],
                    )

        @pl.when(c == 1)
        def _():
            for g in range(groups):
                for r in range(TOKENS // HALF):
                    mine = slice(r * HALF, (r + 1) * HALF)
                    attend(
                        g,
                        r,
                        mine,
                        stacked(g, mine),
                        lambda h, r: split_bias[h, r],
                    )

        x = window[...]
        attended = x + jnp.dot(mix[...], out_w_ref[...], preferred_element_type=jnp.float32)
        normed2 = layer_norm(attended, gain2_ref[...].reshape(1, width)).astype(jnp.bfloat16)
        result = attended
        for j in range(up_ref.shape[1] // UNITS):
            units = slice(j * UNITS, (j + 1) * UNITS)
            feed = gelu(
                jnp.dot(normed2, up_ref[:, units], preferred_element_type=jnp.float32)
            ).astype(jnp.bfloat16)
            result = result + jnp.dot(
                feed, down_ref[units, :], preferred_element_type=jnp.float32
            )
        keep = jnp.concatenate([kept[...]] * groups, axis=1) > 0.5
        result = jnp.where(keep, result, x).astype(jnp.bfloat16)

        @pl.when(c == 0)
        def _():
            half[a] = result

        @pl.when(c == 1)
        def _():
            halves = (
                half[a].astype(jnp.float32),
                jnp.dot(scatter[...], result, preferred_element_type=jnp.float32),
            )
            q = 2 * (1 - b) + 1 - a
            both = jnp.concatenate(
                [part.reshape(SQUARE, WIN, width) for part in halves], axis=1
            )
            both = pltpu.roll(both, SHIFT, 1).astype(jnp.bfloat16)
            done[q] = both.reshape(WIN, WIN, 2 * WIN, width)
            for ph in range(2):
                for rh in range(2):
                    away, direct, remote, inside = back(q, ph, rh)

                    @pl.when(jnp.logical_and(away, b * rh == 0))
                    def _():
                        remote.start()

                    @pl.when(jnp.logical_not(away))
                    def _():
                        inside.start()

            if relayed:

                @pl.when(jnp.logical_and(crossing, q == 0))
                def _():
                    hand_over().start()

    for b in (1, 0):
        for c in (0, 1):

            @pl.loop(1, n_brick)
            def _(j):
                piece(j, b, c)[0].wait_send()

            remote, _ = piece(0, b, c)

            @pl.when(is_early)
            def _():
                remote.wait_send()

    @pl.loop(0, WINDOWS // 2)
    def _(q):
        for ph in range(2):
            for rh in range(2):
                away, direct, remote, inside = back(q, ph, rh)

                @pl.when(away)
                def _():
                    remote.wait_recv()

                @pl.when(jnp.logical_and(away, direct))
                def _():
                    remote.wait_send()

                @pl.when(jnp.logical_not(away))
                def _():
                    inside.wait()

    if relayed:

        @pl.when(crossing)
        def _():
            hand_over().wait_send()

        @pl.when(carrying)
        def _():
            for ph in range(2):
                pass_on(ph).wait_send()


def local(tokens, tissue, gain1, qkv_w, bias, out_w, gain2, up_w, down_w):
    planes, rows, across, width = tokens.shape
    n_sec = lax.axis_size("sec")
    n_brick = lax.axis_size("brick")
    heads = bias.shape[0]
    hbm = pl.BlockSpec(memory_space=pltpu.HBM)
    vmem = pl.BlockSpec(memory_space=pltpu.VMEM)
    parts = across // WIN
    high = planes * n_brick
    wide = rows // n_brick
    return pl.pallas_call(
        functools.partial(
            block_kernel,
            head_size=width // heads,
            n_sec=n_sec,
            n_brick=n_brick,
            relayed=n_brick == 8,
        ),
        out_shape=pltpu.VMEM((high, wide, across, width), jnp.bfloat16),
        in_specs=[hbm, vmem, vmem, hbm, hbm, hbm, vmem, hbm, hbm],
        out_specs=pl.BlockSpec(memory_space=pltpu.VMEM),
        scratch_shapes=[
            pltpu.VMEM(tokens.shape, jnp.bfloat16),
            pltpu.VMEM((rows // WIN, parts, planes, SQUARE, width), jnp.bfloat16),
            pltpu.VMEM((WINDOWS, WIN, SQUARE, width), jnp.bfloat16),
            pltpu.VMEM((2, TOKENS, width), jnp.bfloat16),
            pltpu.VMEM((WINDOWS // 2, WIN, WIN, across, width), jnp.bfloat16),
            pltpu.VMEM((WIN, SHIFT, across, width), jnp.bfloat16),
            pltpu.VMEM(qkv_w.shape, jnp.bfloat16),
            pltpu.VMEM(bias.shape, jnp.bfloat16),
            pltpu.VMEM((heads, 2, HALF, HALF), jnp.bfloat16),
            pltpu.VMEM((TOKENS, TOKENS), jnp.bfloat16),
            pltpu.VMEM((TOKENS, TOKENS), jnp.bfloat16),
            pltpu.VMEM((2, WINDOWS, TOKENS), jnp.float32),
            pltpu.VMEM((TOKENS, width), jnp.float32),
            pltpu.VMEM(out_w.shape, jnp.bfloat16),
            pltpu.VMEM(up_w.shape, jnp.bfloat16),
            pltpu.VMEM(down_w.shape, jnp.bfloat16),
            pltpu.VMEM((TOKENS, 3 * width), jnp.bfloat16),
            pltpu.VMEM((TOKENS, width), jnp.bfloat16),
            pltpu.VMEM((TOKENS, LANES), jnp.bfloat16),
            pltpu.VMEM((TOKENS, LANES), jnp.bfloat16),
            pltpu.VMEM((TOKENS, LANES), jnp.float32),
            pltpu.SemaphoreType.DMA,
            pltpu.SemaphoreType.DMA((5,)),
            pltpu.SemaphoreType.DMA((4, n_brick)),
            pltpu.SemaphoreType.DMA((4, n_brick)),
            pltpu.SemaphoreType.DMA((WINDOWS // 2, 4)),
            pltpu.SemaphoreType.DMA((WINDOWS // 2, 4)),
            pltpu.SemaphoreType.DMA((4,)),
        ],
        compiler_params=pltpu.CompilerParams(
            collective_id=0, has_side_effects=True, vmem_limit_bytes=58 * 2**20
        ),
    )(tokens, tissue, gain1, qkv_w, bias, out_w, gain2, up_w, down_w)


def solution(mesh):
    placed = (
        P(("sec", "brick"), None, None, None),
        P("sec", "brick", None, None),
        P(),
        P(),
        P(),
        P(),
        P(),
        P(),
        P(),
    )
    return jax.shard_map(
        local, mesh=mesh, in_specs=placed, out_specs=P("sec", "brick", None, None), check_vma=False
    )
```
